32 devices in a mesh: parts: 2 (over y), latent: 16 (over z, x, core).
Axes of the slice: x: 2, y: 2, z: 4, core: 2. Of those that a mesh axis runs over, the one named last changes fastest.
Arguments:
- residual: bfloat16 [512, 4608], P(('parts', 'latent')), parts along dimension 0, may hold values from -6 to 6
- enc_weight: bfloat16 [4608, 8192], P(None, 'latent'), may hold values from -0.09375 to 0.09375
- enc_bias: float32 [8192], P('latent'), may hold values from -3 to 3
- threshold: float32 [8192], P('latent'), may hold values from 0.3 to 2
- dec_weight: bfloat16 [8192, 4608], P('latent'), may hold values from -0.1875 to 0.1875
- dec_bias: float32 [4608], replicated, may hold values from -3 to 3
- pre_gain: float32 [4608], replicated, may hold values from 0.1 to 1.9
- gate_weight: bfloat16 [4608, 2304], P(None, 'latent'), may hold values from -0.09375 to 0.09375
- up_weight: bfloat16 [4608, 2304], P(None, 'latent'), may hold values from -0.09375 to 0.09375
- down_weight: bfloat16 [2304, 4608], P('latent'), may hold values from -0.125 to 0.125
- post_gain: float32 [4608], replicated, may hold values from 0.1 to 1.9
Outputs:
- spliced_out: bfloat16 [512, 4608], P(('parts', 'latent')), parts along dimension 0
The draws below stay inside these ranges and needn't reach their ends.
There are 2 independent parts, one for each index of `parts`. The reference program is written for one: setup_inputs(seed, part) draws one part's arguments, and reference() takes and returns one part's arrays. A program takes and returns all parts, laid end to end along the dimension named above; an argument that names none is the same for every part. Nothing has to cross between parts.
All inputs are finite; a program needn't handle non-finite values.
Results may differ from the reference program's by a relative error of at most 0.0057.
Values may be sent and summed in bfloat16 or wider, within the bound.
No kernel may reach another device: no remote copies, remote signals or barrier semaphores. Data moves between devices by JAX's collectives and lax.ppermute only.
A program may use at most 128 MiB of HBM per device.

```python
import math
import jax
import jax.numpy as jnp
from jax import lax

D = 4608
TOK = 256
LATENTS = 8192
FF = 2304


def with_spikes(array, stream_key, source, target, blocks, factor):
    owner, partner = [(jnp.arange(array.shape[position]) // (array.shape[position] // blocks)).reshape([-1 if axis == position else 1 for axis in range(array.ndim)]) for position in (source, target)]
    chosen = jax.random.permutation(stream_key, blocks)[partner]
    strong = (owner == chosen) | (owner == (partner + blocks // 2) % blocks)
    return jnp.where(strong, factor * array, array)


def level_of(stream_key, extent, cuts, smallest, top_value):
    level, own = 1.0, jax.random.fold_in(stream_key, 6)
    for dim, blocks in cuts:
        draws = jnp.exp(jax.random.uniform(jax.random.fold_in(own, dim), (blocks,), jnp.float32, smallest / len(cuts), top_value / len(cuts)))
        level = level * jnp.repeat(draws, extent[dim] // blocks).reshape([-1 if axis == dim else 1 for axis in range(len(extent))])
    return level


def bell_draw(rng, shape, spread, most, cuts=(), held_as=jnp.bfloat16):
    level = level_of(rng, shape, cuts, -0.22, 0.18) if cuts else 1.0
    entries = jax.random.normal(rng, shape, jnp.float32) * spread * level
    return jnp.minimum(jnp.maximum(entries, -most), most).astype(held_as)


def noise_with(stream_key, shape, scale, bound, pieces, heavy, dtype=jnp.bfloat16):
    array = scale * jax.random.normal(stream_key, shape, jnp.float32)
    if pieces:
        array = array * level_of(stream_key, shape, pieces, -0.22, 0.18)
    return jnp.clip(with_spikes(array, jax.random.fold_in(stream_key, 3), *heavy), -bound, bound).astype(dtype)


def setup_inputs(seed: int = 0, part: int = 0) -> dict:
    key_list = jax.random.split(jax.random.key(seed), 12)
    own_keys = jax.random.split(jax.random.fold_in(key_list[11], part), 12)
    return {
        "residual": bell_draw(own_keys[0], (TOK, D), 1.0, 6.0, ((0, 16),)),
        "enc_weight": bell_draw(key_list[1], (D, LATENTS), D ** -0.5, 0.09375, ((1, 16),)),
        "enc_bias": bell_draw(key_list[2], (LATENTS,), 0.5, 3.0, ((0, 16),), jnp.float32),
        "threshold": jnp.clip(jnp.exp(math.log(2.0) - 1.89712 * jax.random.uniform(key_list[3], (LATENTS,), jnp.float32) ** level_of(key_list[3], (LATENTS,), ((0, 16),), -0.2, 0.2)), 0.3, 2.0),
        "dec_weight": noise_with(key_list[4], (LATENTS, D), (LATENTS // 4) ** -0.5, 0.1875, ((0, 16),), (0, 1, 16, 2.0)),
        "dec_bias": bell_draw(key_list[5], (D,), 0.5, 3.0, (), jnp.float32),
        "pre_gain": jnp.clip(1.0 + 0.18 * jax.random.normal(key_list[6], (D,), jnp.float32), 0.1, 1.9),
        "gate_weight": bell_draw(key_list[7], (D, FF), D ** -0.5, 0.09375, ((1, 16),)),
        "up_weight": bell_draw(key_list[8], (D, FF), D ** -0.5, 0.09375, ((1, 16),)),
        "down_weight": bell_draw(key_list[9], (FF, D), FF ** -0.5, 0.125, ((0, 16),)),
        "post_gain": jnp.clip(1.0 + 0.18 * jax.random.normal(key_list[10], (D,), jnp.float32), 0.1, 1.9),
    }


sharpness = 10.0
epsilon = 1e-06

def rms_scale(values, gain):
    return values * jax.lax.rsqrt(lax.optimization_barrier(jnp.mean(values * values, axis=-1, keepdims=True)) + epsilon) * gain

def reference(residual, enc_weight, enc_bias, threshold, dec_weight, dec_bias, pre_gain, gate_weight, up_weight, down_weight, post_gain):
    preact = jnp.dot(residual, enc_weight, preferred_element_type=jnp.float32) + enc_bias
    latent_acts = (preact * jax.nn.sigmoid(sharpness * (preact - threshold))).astype(jnp.bfloat16)
    rebuilt = jnp.dot(latent_acts, dec_weight, preferred_element_type=jnp.float32) + dec_bias
    normed = rms_scale(rebuilt, pre_gain).astype(jnp.bfloat16)
    gate_proj = jnp.dot(normed, gate_weight, preferred_element_type=jnp.float32)
    up_proj = jnp.dot(normed, up_weight, preferred_element_type=jnp.float32)
    hidden = (jax.nn.gelu(gate_proj, approximate=True) * up_proj).astype(jnp.bfloat16)
    ffn_sum = jnp.dot(hidden, down_weight, preferred_element_type=jnp.float32)
    return (rebuilt + rms_scale(ffn_sum, post_gain)).astype(jnp.bfloat16)
```

```python
import jax
import jax.numpy as jnp
from jax import lax
from jax.sharding import PartitionSpec as P

sharpness = 10.0
epsilon = 1e-06
AXIS = "latent"


def inverse_rms(values):
    return lax.rsqrt(jnp.mean(values * values, axis=-1, keepdims=True) + epsilon)


def stages(devices):
    sizes, left = [], devices
    for wanted in (2, max(1, devices // 8), 4):
        size = min(wanted, left)
        sizes.append(size)
        left //= size
    sizes[-1] *= left
    out, stride = [], 1
    for size in sizes:
        out.append((stride, size))
        stride *= size
    return [stage for stage in out if stage[1] > 1]


def exchange(block, offset, devices):
    return lax.ppermute(block, AXIS, [(index, index ^ offset) for index in range(devices)])


def gather_rows(own, devices):
    blocks = [own]
    for stride, size in reversed(stages(devices)):
        blocks = blocks + [exchange(block, stride * k, devices) for k in range(1, size) for block in blocks]
    return jnp.concatenate(blocks, axis=0)


def scatter_rows(total, devices):
    for stride, size in stages(devices):
        rows = total.shape[0] // size
        got = [exchange(total[k * rows : (k + 1) * rows].astype(jnp.bfloat16), stride * k, devices) for k in range(1, size)]
        total = total[:rows]
        for block in got:
            total = total + block.astype(jnp.float32)
    return total


def build(devices):
    def per_device(
        residual,
        enc_weight,
        enc_bias,
        threshold,
        dec_weight,
        dec_bias,
        pre_gain,
        gate_weight,
        up_weight,
        down_weight,
        post_gain,
    ):
        rows = gather_rows(residual, devices)
        preact = jnp.dot(rows, enc_weight, preferred_element_type=jnp.float32) + enc_bias
        latent_acts = (preact * jax.nn.sigmoid(sharpness * (preact - threshold))).astype(jnp.bfloat16)
        rebuilt = scatter_rows(jnp.dot(latent_acts, dec_weight, preferred_element_type=jnp.float32), devices) + dec_bias
        normed = (rebuilt * inverse_rms(rebuilt) * pre_gain).astype(jnp.bfloat16)
        rows = gather_rows(normed, devices)
        gate_proj = jnp.dot(rows, gate_weight, preferred_element_type=jnp.float32)
        up_proj = jnp.dot(rows, up_weight, preferred_element_type=jnp.float32)
        hidden = (jax.nn.gelu(gate_proj, approximate=True) * up_proj).astype(jnp.bfloat16)
        ffn_sum = scatter_rows(jnp.dot(hidden, down_weight, preferred_element_type=jnp.float32), devices)
        return (rebuilt + ffn_sum * inverse_rms(ffn_sum) * post_gain).astype(jnp.bfloat16)

    return per_device


def solution(mesh):
    devices = mesh.shape[AXIS]
    return jax.shard_map(
        build(devices),
        mesh=mesh,
        in_specs=(
            P(("parts", AXIS), None),
            P(None, AXIS),
            P(AXIS),
            P(AXIS),
            P(AXIS, None),
            P(),
            P(),
            P(None, AXIS),
            P(None, AXIS),
            P(AXIS, None),
            P(),
        ),
        out_specs=P(("parts", AXIS), None),
        check_vma=False,
    )
```

```python
import jax
import jax.numpy as jnp
from jax import lax
from jax.sharding import PartitionSpec as P

sharpness = 10.0
epsilon = 1e-06
AXIS = "latent"
LANES = 128
CHUNKS = 2


def stages(devices):
    sizes, left = [], devices
    for wanted in (2, max(1, devices // 8), 4):
        size = min(wanted, left)
        sizes.append(size)
        left //= size
    sizes[-1] *= left
    out, stride = [], 1
    for size in sizes:
        out.append((stride, size))
        stride *= size
    return [stage for stage in out if stage[1] > 1]


def exchange(block, offset, devices):
    return lax.ppermute(block, AXIS, [(index, index ^ offset) for index in range(devices)])


def gather_rows(own, devices):
    blocks = [own]
    for stride, size in reversed(stages(devices)):
        blocks = blocks + [exchange(block, stride * k, devices) for k in range(1, size) for block in blocks]
    return jnp.concatenate(blocks, axis=0)


def gather_rows_whole(own, devices):
    rows = own
    for stride, size in reversed(stages(devices)):
        rows = jnp.concatenate([rows] + [exchange(rows, stride * k, devices) for k in range(1, size)], axis=0)
    return rows


def scatter_rows(total, devices):
    for stride, size in stages(devices):
        rows = total.shape[0] // size
        got = [exchange(total[k * rows : (k + 1) * rows].astype(jnp.bfloat16), stride * k, devices) for k in range(1, size)]
        total = total[:rows]
        for block in got:
            total = total + block.astype(jnp.float32)
    return total


def column_chunks(width):
    lanes = -(-width // (LANES * CHUNKS)) * LANES
    return [(start, min(start + lanes, width)) for start in range(0, width, lanes)]


def build(devices):
    def per_device(
        residual,
        enc_weight,
        enc_bias,
        threshold,
        dec_weight,
        dec_bias,
        pre_gain,
        gate_weight,
        up_weight,
        down_weight,
        post_gain,
    ):
        width = residual.shape[1]
        chunks = column_chunks(width)
        rows = gather_rows(residual, devices)
        preact = jnp.dot(rows, enc_weight, preferred_element_type=jnp.float32) + enc_bias
        latent_acts = (preact * jax.nn.sigmoid(sharpness * (preact - threshold))).astype(jnp.bfloat16)
        latent_acts = lax.optimization_barrier(latent_acts)

        rebuilt, squares, gate_proj, up_proj = [], 0.0, 0.0, 0.0
        for start, stop in chunks:
            part = jnp.dot(latent_acts, dec_weight[:, start:stop], preferred_element_type=jnp.float32)
            part = scatter_rows(part, devices) + dec_bias[start:stop]
            rebuilt.append(part)
            squares = squares + jnp.sum(part * part, axis=-1, keepdims=True)
            sent = (part * pre_gain[start:stop]).astype(jnp.bfloat16)
            if stop == width:
                scale = lax.rsqrt(squares / width + epsilon)
                high = scale.astype(jnp.bfloat16)
                low = (scale - high.astype(jnp.float32)).astype(jnp.bfloat16)
                lane = lax.broadcasted_iota(jnp.int32, (sent.shape[0], LANES), 1)
                sent = jnp.concatenate([sent, jnp.where(lane == 0, high, low)], axis=1)
            rows = gather_rows_whole(sent, devices)
            if stop == width:
                tail = rows[:, stop - start :].astype(jnp.float32)
                scale = tail[:, 0:1] + tail[:, 1:2]
                rows = rows[:, : stop - start]
            gate_proj = gate_proj + jnp.dot(rows, gate_weight[start:stop], preferred_element_type=jnp.float32)
            up_proj = up_proj + jnp.dot(rows, up_weight[start:stop], preferred_element_type=jnp.float32)

        hidden = (jax.nn.gelu(gate_proj * scale, approximate=True) * (up_proj * scale)).astype(jnp.bfloat16)
        hidden = lax.optimization_barrier(hidden)

        ffn_sum, squares = [], 0.0
        for start, stop in chunks:
            part = jnp.dot(hidden, down_weight[:, start:stop], preferred_element_type=jnp.float32)
            part = scatter_rows(part, devices)
            ffn_sum.append(part)
            squares = squares + jnp.sum(part * part, axis=-1, keepdims=True)
        scale = lax.rsqrt(squares / width + epsilon)
        out = [
            (kept + part * scale * post_gain[start:stop]).astype(jnp.bfloat16)
            for (start, stop), kept, part in zip(chunks, rebuilt, ffn_sum)
        ]
        return jnp.concatenate(out, axis=1)

    return per_device


def solution(mesh):
    devices = mesh.shape[AXIS]
    return jax.shard_map(
        build(devices),
        mesh=mesh,
        in_specs=(
            P(("parts", AXIS), None),
            P(None, AXIS),
            P(AXIS),
            P(AXIS),
            P(AXIS, None),
            P(),
            P(),
            P(None, AXIS),
            P(None, AXIS),
            P(AXIS, None),
            P(),
        ),
        out_specs=P(("parts", AXIS), None),
        check_vma=False,
    )
```

```python
import jax
import jax.numpy as jnp
from jax import lax
from jax.sharding import PartitionSpec as P

sharpness = 10.0
epsilon = 1e-06
AXIS = "latent"
LANES = 128
IN_SPLIT = 2
MID_SPLIT = 4
BACK_SPLIT = 4
OUT_SPLIT = 4
MID_CHUNKS = (4, 4, 4)
OUT_CHUNKS = (6, 6)


def stages(devices, split):
    sizes, left = [], devices
    for wanted in (2, max(1, devices // 8)):
        size = min(wanted, left)
        sizes.append(size)
        left //= size
    while left > 1:
        size = min(split, left)
        sizes.append(size)
        left //= size
    out, stride = [], 1
    for size in sizes:
        out.append((stride, size))
        stride *= size
    return [stage for stage in out if stage[1] > 1]


def exchange(block, offset, devices):
    return lax.ppermute(block, AXIS, [(index, index ^ offset) for index in range(devices)])


def gather_rows(own, devices):
    blocks = {0: own}
    for stride, size in reversed(stages(devices, IN_SPLIT)):
        for offset, block in list(blocks.items()):
            for k in range(1, size):
                blocks[offset + stride * k] = exchange(block, stride * k, devices)
    order = [0]
    for stride, size in reversed(stages(devices, MID_SPLIT)):
        order = [offset + stride * k for k in range(size) for offset in order]
    return jnp.concatenate([blocks[offset] for offset in order], axis=0)


def gather_rows_whole(own, devices):
    rows = own
    for stride, size in reversed(stages(devices, BACK_SPLIT)):
        rows = jnp.concatenate([rows] + [exchange(rows, stride * k, devices) for k in range(1, size)], axis=0)
    return rows


def scatter_rows(total, devices, split):
    for stride, size in stages(devices, split):
        rows = total.shape[0] // size
        got = [exchange(total[k * rows : (k + 1) * rows].astype(jnp.bfloat16), stride * k, devices) for k in range(1, size)]
        total = total[:rows]
        for block in got:
            total = total + block.astype(jnp.float32)
    return total


def column_chunks(width, shares):
    out, start, seen = [], 0, 0
    for share in shares:
        seen += share
        stop = width if seen == sum(shares) else width * seen // (sum(shares) * LANES) * LANES
        if stop > start:
            out.append((start, stop))
        start = stop
    return out


def build(devices):
    def per_device(
        residual,
        enc_weight,
        enc_bias,
        threshold,
        dec_weight,
        dec_bias,
        pre_gain,
        gate_weight,
        up_weight,
        down_weight,
        post_gain,
    ):
        width = residual.shape[1]
        rows = gather_rows(residual, devices)
        preact = jnp.dot(rows, enc_weight, preferred_element_type=jnp.float32) + enc_bias
        latent_acts = (preact * jax.nn.sigmoid(sharpness * (preact - threshold))).astype(jnp.bfloat16)
        latent_acts = lax.optimization_barrier(latent_acts)

        rebuilt, squares, gate_proj, up_proj = [], 0.0, 0.0, 0.0
        for start, stop in column_chunks(width, MID_CHUNKS):
            part = jnp.dot(latent_acts, dec_weight[:, start:stop], preferred_element_type=jnp.float32)
            part = scatter_rows(part, devices, MID_SPLIT) + dec_bias[start:stop]
            rebuilt.append(part)
            squares = squares + jnp.sum(part * part, axis=-1, keepdims=True)
            sent = (part * pre_gain[start:stop]).astype(jnp.bfloat16)
            if stop == width:
                scale = lax.rsqrt(squares / width + epsilon)
                high = scale.astype(jnp.bfloat16)
                low = (scale - high.astype(jnp.float32)).astype(jnp.bfloat16)
                lane = lax.broadcasted_iota(jnp.int32, (sent.shape[0], LANES), 1)
                sent = jnp.concatenate([sent, jnp.where(lane == 0, high, low)], axis=1)
            rows = gather_rows_whole(sent, devices)
            if stop == width:
                tail = rows[:, stop - start :].astype(jnp.float32)
                scale = tail[:, 0:1] + tail[:, 1:2]
                rows = rows[:, : stop - start]
            gate_proj = gate_proj + jnp.dot(rows, gate_weight[start:stop], preferred_element_type=jnp.float32)
            up_proj = up_proj + jnp.dot(rows, up_weight[start:stop], preferred_element_type=jnp.float32)

        hidden = (jax.nn.gelu(gate_proj * scale, approximate=True) * (up_proj * scale)).astype(jnp.bfloat16)
        hidden = lax.optimization_barrier(hidden)

        rebuilt = jnp.concatenate(rebuilt, axis=1)
        ffn_sum = []
        for start, stop in column_chunks(width, OUT_CHUNKS):
            part = jnp.dot(hidden, down_weight[:, start:stop], preferred_element_type=jnp.float32)
            ffn_sum.append(scatter_rows(part, devices, OUT_SPLIT))
        ffn_sum = jnp.concatenate(ffn_sum, axis=1)
        scale = lax.rsqrt(jnp.mean(ffn_sum * ffn_sum, axis=-1, keepdims=True) + epsilon)
        return (rebuilt + ffn_sum * scale * post_gain).astype(jnp.bfloat16)

    return per_device


def solution(mesh):
    devices = mesh.shape[AXIS]
    return jax.shard_map(
        build(devices),
        mesh=mesh,
        in_specs=(
            P(("parts", AXIS), None),
            P(None, AXIS),
            P(AXIS),
            P(AXIS),
            P(AXIS, None),
            P(),
            P(),
            P(None, AXIS),
            P(None, AXIS),
            P(AXIS, None),
            P(),
        ),
        out_specs=P(("parts", AXIS), None),
        check_vma=False,
    )
```

```python
import jax
import jax.numpy as jnp
from jax import lax
from jax.sharding import PartitionSpec as P

sharpness = 10.0
epsilon = 1e-06
AXIS = "latent"
LANES = 128
IN_PIECES = 16
BACK_PIECES = 1
MID_CHUNKS = (4, 4, 4)
OUT_CHUNKS = (6, 6)


def swaps(stage, devices):
    bits = list(range(devices.bit_length() - 1))
    other = bits[:1] + bits[2:3] + bits[1:2] + bits[3:]
    return [(index, index ^ (1 << (other if index & 1 else bits)[stage])) for index in range(devices)]


def exchange(block, stage, devices):
    return lax.ppermute(block, AXIS, swaps(stage, devices))


def gather_rows(own, devices, pieces):
    blocks = [own]
    for stage in reversed(range(devices.bit_length() - 1)):
        blocks = blocks + [exchange(block, stage, devices) for block in blocks]
        if len(blocks) > pieces:
            blocks = [jnp.concatenate(blocks, axis=0)]
    return jnp.concatenate(blocks, axis=0)


def scatter_rows(total, devices):
    for stage in range(devices.bit_length() - 1):
        rows = total.shape[0] // 2
        got = exchange(total[rows:].astype(jnp.bfloat16), stage, devices)
        total = total[:rows] + got.astype(jnp.float32)
    return total


def column_chunks(width, shares):
    out, start, seen = [], 0, 0
    for share in shares:
        seen += share
        stop = width if seen == sum(shares) else width * seen // (sum(shares) * LANES) * LANES
        if stop > start:
            out.append((start, stop))
        start = stop
    return out


def build(devices):
    def per_device(
        residual,
        enc_weight,
        enc_bias,
        threshold,
        dec_weight,
        dec_bias,
        pre_gain,
        gate_weight,
        up_weight,
        down_weight,
        post_gain,
    ):
        width = residual.shape[1]
        rows = gather_rows(residual, devices, IN_PIECES)
        preact = jnp.dot(rows, enc_weight, preferred_element_type=jnp.float32) + enc_bias
        latent_acts = (preact * jax.nn.sigmoid(sharpness * (preact - threshold))).astype(jnp.bfloat16)
        latent_acts = lax.optimization_barrier(latent_acts)

        rebuilt, squares, gate_proj, up_proj = [], 0.0, 0.0, 0.0
        for start, stop in column_chunks(width, MID_CHUNKS):
            part = jnp.dot(latent_acts, dec_weight[:, start:stop], preferred_element_type=jnp.float32)
            part = scatter_rows(part, devices) + dec_bias[start:stop]
            rebuilt.append(part)
            squares = squares + jnp.sum(part * part, axis=-1, keepdims=True)
            sent = (part * pre_gain[start:stop]).astype(jnp.bfloat16)
            if stop == width:
                scale = lax.rsqrt(squares / width + epsilon)
                high = scale.astype(jnp.bfloat16)
                low = (scale - high.astype(jnp.float32)).astype(jnp.bfloat16)
                lane = lax.broadcasted_iota(jnp.int32, (sent.shape[0], LANES), 1)
                sent = jnp.concatenate([sent, jnp.where(lane == 0, high, low)], axis=1)
            rows = gather_rows(sent, devices, BACK_PIECES)
            if stop == width:
                tail = rows[:, stop - start :].astype(jnp.float32)
                scale = tail[:, 0:1] + tail[:, 1:2]
                rows = rows[:, : stop - start]
            gate_proj = gate_proj + jnp.dot(rows, gate_weight[start:stop], preferred_element_type=jnp.float32)
            up_proj = up_proj + jnp.dot(rows, up_weight[start:stop], preferred_element_type=jnp.float32)

        hidden = (jax.nn.gelu(gate_proj * scale, approximate=True) * (up_proj * scale)).astype(jnp.bfloat16)
        hidden = lax.optimization_barrier(hidden)

        rebuilt = jnp.concatenate(rebuilt, axis=1)
        ffn_sum = []
        for start, stop in column_chunks(width, OUT_CHUNKS):
            part = jnp.dot(hidden, down_weight[:, start:stop], preferred_element_type=jnp.float32)
            ffn_sum.append(scatter_rows(part, devices))
        ffn_sum = jnp.concatenate(ffn_sum, axis=1)
        scale = lax.rsqrt(jnp.mean(ffn_sum * ffn_sum, axis=-1, keepdims=True) + epsilon)
        return (rebuilt + ffn_sum * scale * post_gain).astype(jnp.bfloat16)

    return per_device


def solution(mesh):
    devices = mesh.shape[AXIS]
    return jax.shard_map(
        build(devices),
        mesh=mesh,
        in_specs=(
            P(("parts", AXIS), None),
            P(None, AXIS),
            P(AXIS),
            P(AXIS),
            P(AXIS, None),
            P(),
            P(),
            P(None, AXIS),
            P(None, AXIS),
            P(AXIS, None),
            P(),
        ),
        out_specs=P(("parts", AXIS), None),
        check_vma=False,
    )
```

```python
import jax
import jax.numpy as jnp
from jax import lax
from jax.sharding import PartitionSpec as P

sharpness = 10.0
epsilon = 1e-06
AXIS = "latent"
LANES = 128
IN_PIECES = 2
MID_CHUNKS = (4, 4, 4)
OUT_CHUNKS = (11, 7)


def swaps(stage, devices):
    bits = list(range(devices.bit_length() - 1))
    other = bits[:1] + bits[2:3] + bits[1:2] + bits[3:]
    return [(index, index ^ (1 << (other if index & 1 else bits)[stage])) for index in range(devices)]


def exchange(block, stage, devices):
    return lax.ppermute(block, AXIS, swaps(stage, devices))


def exchange_both(block, devices):
    return lax.ppermute(block, AXIS, [(index, index ^ 6) for index in range(devices)])


def gather_pieces(own, devices):
    bits = devices.bit_length() - 1
    if bits < 3:
        return gather_rows(own, devices)
    blocks = [own]
    for stage in reversed(range(3, bits)):
        blocks = blocks + [exchange(block, stage, devices) for block in blocks]
        if len(blocks) > IN_PIECES:
            blocks = [jnp.concatenate(blocks, axis=0)]
    across = [[exchange(block, stage, devices) for block in blocks] for stage in (2, 1)]
    blocks = blocks + across[0] + across[1] + [exchange_both(block, devices) for block in blocks]
    return jnp.concatenate(blocks + [exchange(block, 0, devices) for block in blocks], axis=0)


def gather_rows(own, devices):
    for stage in reversed(range(devices.bit_length() - 1)):
        own = jnp.concatenate([own, exchange(own, stage, devices)], axis=0)
    return own


def scatter_rows(total, devices):
    for stage in range(devices.bit_length() - 1):
        rows = total.shape[0] // 2
        got = exchange(total[rows:].astype(jnp.bfloat16), stage, devices)
        total = total[:rows] + got.astype(jnp.float32)
    return total


def column_chunks(width, shares):
    out, start, seen = [], 0, 0
    for share in shares:
        seen += share
        stop = width if seen == sum(shares) else width * seen // (sum(shares) * LANES) * LANES
        if stop > start:
            out.append((start, stop))
        start = stop
    return out


def build(devices):
    def per_device(
        residual,
        enc_weight,
        enc_bias,
        threshold,
        dec_weight,
        dec_bias,
        pre_gain,
        gate_weight,
        up_weight,
        down_weight,
        post_gain,
    ):
        width = residual.shape[1]
        rows = gather_pieces(residual, devices)
        preact = jnp.dot(rows, enc_weight, preferred_element_type=jnp.float32) + enc_bias
        latent_acts = (preact * jax.nn.sigmoid(sharpness * (preact - threshold))).astype(jnp.bfloat16)
        latent_acts = lax.optimization_barrier(latent_acts)

        rebuilt, squares, gate_proj, up_proj = [], 0.0, 0.0, 0.0
        for start, stop in column_chunks(width, MID_CHUNKS):
            part = jnp.dot(latent_acts, dec_weight[:, start:stop], preferred_element_type=jnp.float32)
            part = scatter_rows(part, devices) + dec_bias[start:stop]
            rebuilt.append(part)
            squares = squares + jnp.sum(part * part, axis=-1, keepdims=True)
            sent = (part * pre_gain[start:stop]).astype(jnp.bfloat16)
            if stop == width:
                scale = lax.rsqrt(squares / width + epsilon)
                high = scale.astype(jnp.bfloat16)
                low = (scale - high.astype(jnp.float32)).astype(jnp.bfloat16)
                lane = lax.broadcasted_iota(jnp.int32, (sent.shape[0], LANES), 1)
                sent = jnp.concatenate([sent, jnp.where(lane == 0, high, low)], axis=1)
            rows = gather_rows(sent, devices)
            if stop == width:
                tail = rows[:, stop - start :].astype(jnp.float32)
                scale = tail[:, 0:1] + tail[:, 1:2]
                rows = rows[:, : stop - start]
            gate_proj = gate_proj + jnp.dot(rows, gate_weight[start:stop], preferred_element_type=jnp.float32)
            up_proj = up_proj + jnp.dot(rows, up_weight[start:stop], preferred_element_type=jnp.float32)

        hidden = (jax.nn.gelu(gate_proj * scale, approximate=True) * (up_proj * scale)).astype(jnp.bfloat16)
        hidden = lax.optimization_barrier(hidden)

        rebuilt = jnp.concatenate(rebuilt, axis=1)
        ffn_sum = []
        for start, stop in column_chunks(width, OUT_CHUNKS):
            part = jnp.dot(hidden, down_weight[:, start:stop], preferred_element_type=jnp.float32)
            ffn_sum.append(scatter_rows(part, devices))
        ffn_sum = jnp.concatenate(ffn_sum, axis=1)
        scale = lax.rsqrt(jnp.mean(ffn_sum * ffn_sum, axis=-1, keepdims=True) + epsilon)
        return (rebuilt + ffn_sum * scale * post_gain).astype(jnp.bfloat16)

    return per_device


def solution(mesh):
    devices = mesh.shape[AXIS]
    return jax.shard_map(
        build(devices),
        mesh=mesh,
        in_specs=(
            P(("parts", AXIS), None),
            P(None, AXIS),
            P(AXIS),
            P(AXIS),
            P(AXIS, None),
            P(),
            P(),
            P(None, AXIS),
            P(None, AXIS),
            P(AXIS, None),
            P(),
        ),
        out_specs=P(("parts", AXIS), None),
        check_vma=False,
    )
```

```python
import jax
import jax.numpy as jnp
from jax import lax
from jax.sharding import PartitionSpec as P

sharpness = 10.0
epsilon = 1e-06
AXIS = "latent"
LANES = 128
IN_PIECES = 2
MID_CHUNKS = (4, 4, 4)
OUT_CHUNKS = (4, 4, 4)


def swaps(stage, devices):
    bits = list(range(devices.bit_length() - 1))
    other = bits[:1] + bits[2:3] + bits[1:2] + bits[3:]
    return [(index, index ^ (1 << (other if index & 1 else bits)[stage])) for index in range(devices)]


def exchange(block, stage, devices):
    return lax.ppermute(block, AXIS, swaps(stage, devices))


def exchange_both(block, devices):
    return lax.ppermute(block, AXIS, [(index, index ^ 6) for index in range(devices)])


def gather_pieces(own, devices):
    bits = devices.bit_length() - 1
    if bits < 3:
        return gather_rows(own, devices)
    blocks = [own]
    for stage in reversed(range(3, bits)):
        blocks = blocks + [exchange(block, stage, devices) for block in blocks]
        if len(blocks) > IN_PIECES:
            blocks = [jnp.concatenate(blocks, axis=0)]
    across = [[exchange(block, stage, devices) for block in blocks] for stage in (2, 1)]
    blocks = blocks + across[0] + across[1] + [exchange_both(block, devices) for block in blocks]
    return jnp.concatenate(blocks + [exchange(block, 0, devices) for block in blocks], axis=0)


def gather_rows(own, devices):
    for stage in reversed(range(devices.bit_length() - 1)):
        own = jnp.concatenate([own, exchange(own, stage, devices)], axis=0)
    return own


def scatter_rows(total, devices):
    for stage in range(devices.bit_length() - 1):
        rows = total.shape[0] // 2
        got = exchange(total[rows:].astype(jnp.bfloat16), stage, devices)
        total = total[:rows] + got.astype(jnp.float32)
    return total


def scatter_all(totals, devices):
    for stage in range(devices.bit_length() - 1):
        rows = totals[0].shape[0] // 2
        gots = [exchange(total[rows:].astype(jnp.bfloat16), stage, devices) for total in totals]
        totals = [total[:rows] + got.astype(jnp.float32) for total, got in zip(totals, gots)]
    return totals


def column_chunks(width, shares):
    out, start, seen = [], 0, 0
    for share in shares:
        seen += share
        stop = width if seen == sum(shares) else width * seen // (sum(shares) * LANES) * LANES
        if stop > start:
            out.append((start, stop))
        start = stop
    return out


def build(devices):
    def per_device(
        residual,
        enc_weight,
        enc_bias,
        threshold,
        dec_weight,
        dec_bias,
        pre_gain,
        gate_weight,
        up_weight,
        down_weight,
        post_gain,
    ):
        width = residual.shape[1]
        rows = gather_pieces(residual, devices)
        preact = jnp.dot(rows, enc_weight, preferred_element_type=jnp.float32) + enc_bias
        latent_acts = (preact * jax.nn.sigmoid(sharpness * (preact - threshold))).astype(jnp.bfloat16)
        latent_acts = lax.optimization_barrier(latent_acts)

        spans = column_chunks(width, MID_CHUNKS)
        sums = [jnp.dot(latent_acts, dec_weight[:, lo:hi], preferred_element_type=jnp.float32) for lo, hi in spans]
        rebuilt = [part + dec_bias[lo:hi] for part, (lo, hi) in zip(scatter_all(sums, devices), spans)]
        squares = sum(jnp.sum(part * part, axis=-1, keepdims=True) for part in rebuilt)
        sends = [(part * pre_gain[lo:hi]).astype(jnp.bfloat16) for part, (lo, hi) in zip(rebuilt, spans)]
        scale = lax.rsqrt(squares / width + epsilon)
        high = scale.astype(jnp.bfloat16)
        low = (scale - high.astype(jnp.float32)).astype(jnp.bfloat16)
        lane = lax.broadcasted_iota(jnp.int32, (high.shape[0], LANES), 1)
        sends[-1] = jnp.concatenate([sends[-1], jnp.where(lane == 0, high, low)], axis=1)
        for stage in reversed(range(devices.bit_length() - 1)):
            sends = [jnp.concatenate([block, exchange(block, stage, devices)], axis=0) for block in sends]
        tail = sends[-1][:, -LANES:].astype(jnp.float32)
        scale = tail[:, 0:1] + tail[:, 1:2]
        sends[-1] = sends[-1][:, :-LANES]
        gate_proj = up_proj = 0.0
        for rows, (lo, hi) in zip(sends, spans):
            gate_proj = gate_proj + jnp.dot(rows, gate_weight[lo:hi], preferred_element_type=jnp.float32)
            up_proj = up_proj + jnp.dot(rows, up_weight[lo:hi], preferred_element_type=jnp.float32)

        hidden = (jax.nn.gelu(gate_proj * scale, approximate=True) * (up_proj * scale)).astype(jnp.bfloat16)
        hidden = lax.optimization_barrier(hidden)

        rebuilt = jnp.concatenate(rebuilt, axis=1)
        spans = column_chunks(width, OUT_CHUNKS)
        sums = [jnp.dot(hidden, down_weight[:, lo:hi], preferred_element_type=jnp.float32) for lo, hi in spans]
        ffn_sum = scatter_all(sums, devices)
        ffn_sum = jnp.concatenate(ffn_sum, axis=1)
        scale = lax.rsqrt(jnp.mean(ffn_sum * ffn_sum, axis=-1, keepdims=True) + epsilon)
        return (rebuilt + ffn_sum * scale * post_gain).astype(jnp.bfloat16)

    return per_device


def solution(mesh):
    devices = mesh.shape[AXIS]
    return jax.shard_map(
        build(devices),
        mesh=mesh,
        in_specs=(
            P(("parts", AXIS), None),
            P(None, AXIS),
            P(AXIS),
            P(AXIS),
            P(AXIS, None),
            P(),
            P(),
            P(None, AXIS),
            P(None, AXIS),
            P(AXIS, None),
            P(),
        ),
        out_specs=P(("parts", AXIS), None),
        check_vma=False,
    )
```

```python
import jax
import jax.numpy as jnp
from jax import lax
from jax.sharding import PartitionSpec as P

sharpness = 10.0
epsilon = 1e-06
AXIS = "latent"
LANES = 128
IN_PIECES = 2
MID_CHUNKS = (4, 4, 4)
OUT_CHUNKS = (4, 4, 4)


def swaps(stage, devices):
    bits = list(range(devices.bit_length() - 1))
    other = bits[:1] + bits[2:3] + bits[1:2] + bits[3:]
    return [(index, index ^ (1 << (other if index & 1 else bits)[stage])) for index in range(devices)]


def exchange(block, stage, devices):
    return lax.ppermute(block, AXIS, swaps(stage, devices))


def exchange_both(block, devices):
    return lax.ppermute(block, AXIS, [(index, index ^ 6) for index in range(devices)])


def gather_pieces(own, devices):
    bits = devices.bit_length() - 1
    if bits < 3:
        return gather_rows(own, devices)
    blocks = [own]
    for stage in reversed(range(3, bits)):
        blocks = blocks + [exchange(block, stage, devices) for block in blocks]
        if len(blocks) > IN_PIECES:
            blocks = [jnp.concatenate(blocks, axis=0)]
    across = [[exchange(block, stage, devices) for block in blocks] for stage in (2, 1)]
    blocks = blocks + across[0] + across[1] + [exchange_both(block, devices) for block in blocks]
    return jnp.concatenate(blocks + [exchange(block, 0, devices) for block in blocks], axis=0)


def gather_rows(own, devices):
    for stage in reversed(range(devices.bit_length() - 1)):
        own = jnp.concatenate([own, exchange(own, stage, devices)], axis=0)
    return own


def scatter_rows(total, devices):
    for stage in range(devices.bit_length() - 1):
        rows = total.shape[0] // 2
        got = exchange(total[rows:].astype(jnp.bfloat16), stage, devices)
        total = total[:rows] + got.astype(jnp.float32)
    return total


def scatter_all(totals, devices):
    for stage in range(devices.bit_length() - 1):
        rows = totals[0].shape[0] // 2
        gots = [exchange(total[rows:].astype(jnp.bfloat16), stage, devices) for total in totals]
        totals = [total[:rows] + got.astype(jnp.float32) for total, got in zip(totals, gots)]
    return totals


def column_chunks(width, shares):
    out, start, seen = [], 0, 0
    for share in shares:
        seen += share
        stop = width if seen == sum(shares) else width * seen // (sum(shares) * LANES) * LANES
        if stop > start:
            out.append((start, stop))
        start = stop
    return out


def build(devices):
    def per_device(
        residual,
        enc_weight,
        enc_bias,
        threshold,
        dec_weight,
        dec_bias,
        pre_gain,
        gate_weight,
        up_weight,
        down_weight,
        post_gain,
    ):
        width = residual.shape[1]
        rows = gather_pieces(residual, devices)
        preact = jnp.dot(rows, enc_weight, preferred_element_type=jnp.float32) + enc_bias
        latent_acts = (preact * jax.nn.sigmoid(sharpness * (preact - threshold))).astype(jnp.bfloat16)

        spans = column_chunks(width, MID_CHUNKS)
        sums = [jnp.dot(latent_acts, dec_weight[:, lo:hi], preferred_element_type=jnp.float32) for lo, hi in spans]
        rebuilt = [part + dec_bias[lo:hi] for part, (lo, hi) in zip(scatter_all(sums, devices), spans)]
        squares = sum(jnp.sum(part * part, axis=-1, keepdims=True) for part in rebuilt)
        sends = [(part * pre_gain[lo:hi]).astype(jnp.bfloat16) for part, (lo, hi) in zip(rebuilt, spans)]
        scale = lax.rsqrt(squares / width + epsilon)
        high = scale.astype(jnp.bfloat16)
        low = (scale - high.astype(jnp.float32)).astype(jnp.bfloat16)
        lane = lax.broadcasted_iota(jnp.int32, (high.shape[0], LANES), 1)
        sends[-1] = jnp.concatenate([sends[-1], jnp.where(lane == 0, high, low)], axis=1)
        for stage in reversed(range(devices.bit_length() - 1)):
            sends = [jnp.concatenate([block, exchange(block, stage, devices)], axis=0) for block in sends]
        tail = sends[-1][:, -LANES:].astype(jnp.float32)
        scale = tail[:, 0:1] + tail[:, 1:2]
        sends[-1] = sends[-1][:, :-LANES]
        gate_proj = up_proj = 0.0
        for rows, (lo, hi) in zip(sends, spans):
            gate_proj = gate_proj + jnp.dot(rows, gate_weight[lo:hi], preferred_element_type=jnp.float32)
            up_proj = up_proj + jnp.dot(rows, up_weight[lo:hi], preferred_element_type=jnp.float32)

        hidden = (jax.nn.gelu(gate_proj * scale, approximate=True) * (up_proj * scale)).astype(jnp.bfloat16)

        rebuilt = jnp.concatenate(rebuilt, axis=1)
        spans = column_chunks(width, OUT_CHUNKS)
        sums = [jnp.dot(hidden, down_weight[:, lo:hi], preferred_element_type=jnp.float32) for lo, hi in spans]
        ffn_sum = scatter_all(sums, devices)
        ffn_sum = jnp.concatenate(ffn_sum, axis=1)
        scale = lax.rsqrt(jnp.mean(ffn_sum * ffn_sum, axis=-1, keepdims=True) + epsilon)
        return (rebuilt + ffn_sum * scale * post_gain).astype(jnp.bfloat16)

    return per_device


def solution(mesh):
    devices = mesh.shape[AXIS]
    return jax.shard_map(
        build(devices),
        mesh=mesh,
        in_specs=(
            P(("parts", AXIS), None),
            P(None, AXIS),
            P(AXIS),
            P(AXIS),
            P(AXIS, None),
            P(),
            P(),
            P(None, AXIS),
            P(None, AXIS),
            P(AXIS, None),
            P(),
        ),
        out_specs=P(("parts", AXIS), None),
        check_vma=False,
    )
```

```python
import jax
import jax.numpy as jnp
from jax import lax
from jax.sharding import PartitionSpec as P

sharpness = 10.0
epsilon = 1e-06
AXIS = "latent"
LANES = 128
IN_PIECES = 2
MID_CHUNKS = (4, 4, 4)
OUT_CHUNKS = (11, 7)


def swaps(stage, devices):
    bits = list(range(devices.bit_length() - 1))
    other = bits[:1] + bits[2:3] + bits[1:2] + bits[3:]
    return [(index, index ^ (1 << (other if index & 1 else bits)[stage])) for index in range(devices)]


def exchange(block, stage, devices):
    return lax.ppermute(block, AXIS, swaps(stage, devices))


def exchange_both(block, devices):
    return lax.ppermute(block, AXIS, [(index, index ^ 6) for index in range(devices)])


def gather_pieces(own, devices):
    bits = devices.bit_length() - 1
    if bits < 3:
        return gather_rows(own, devices)
    blocks = [own]
    for stage in reversed(range(3, bits)):
        blocks = blocks + [exchange(block, stage, devices) for block in blocks]
        if len(blocks) > IN_PIECES:
            blocks = [jnp.concatenate(blocks, axis=0)]
    across = [[exchange(block, stage, devices) for block in blocks] for stage in (2, 1)]
    blocks = blocks + across[0] + across[1] + [exchange_both(block, devices) for block in blocks]
    return jnp.concatenate(blocks + [exchange(block, 0, devices) for block in blocks], axis=0)


def gather_rows(own, devices):
    for stage in reversed(range(devices.bit_length() - 1)):
        own = jnp.concatenate([own, exchange(own, stage, devices)], axis=0)
    return own


def scatter_rows(total, devices):
    for stage in range(devices.bit_length() - 1):
        rows = total.shape[0] // 2
        got = exchange(total[rows:].astype(jnp.bfloat16), stage, devices)
        total = total[:rows] + got.astype(jnp.float32)
    return total


def scatter_all(totals, devices):
    for stage in range(devices.bit_length() - 1):
        rows = totals[0].shape[0] // 2
        gots = [exchange(total[rows:].astype(jnp.bfloat16), stage, devices) for total in totals]
        totals = [total[:rows] + got.astype(jnp.float32) for total, got in zip(totals, gots)]
    return totals


def column_chunks(width, shares):
    out, start, seen = [], 0, 0
    for share in shares:
        seen += share
        stop = width if seen == sum(shares) else width * seen // (sum(shares) * LANES) * LANES
        if stop > start:
            out.append((start, stop))
        start = stop
    return out


def build(devices):
    def per_device(
        residual,
        enc_weight,
        enc_bias,
        threshold,
        dec_weight,
        dec_bias,
        pre_gain,
        gate_weight,
        up_weight,
        down_weight,
        post_gain,
    ):
        width = residual.shape[1]
        rows = gather_pieces(residual, devices)
        preact = jnp.dot(rows, enc_weight, preferred_element_type=jnp.float32) + enc_bias
        latent_acts = (preact * jax.nn.sigmoid(sharpness * (preact - threshold))).astype(jnp.bfloat16)
        latent_acts = lax.optimization_barrier(latent_acts)

        spans = column_chunks(width, MID_CHUNKS)
        sums = [jnp.dot(latent_acts, dec_weight[:, lo:hi], preferred_element_type=jnp.float32) for lo, hi in spans]
        rebuilt = [part + dec_bias[lo:hi] for part, (lo, hi) in zip(scatter_all(sums, devices), spans)]
        squares = sum(jnp.sum(part * part, axis=-1, keepdims=True) for part in rebuilt)
        sends = [(part * pre_gain[lo:hi]).astype(jnp.bfloat16) for part, (lo, hi) in zip(rebuilt, spans)]
        scale = lax.rsqrt(squares / width + epsilon)
        high = scale.astype(jnp.bfloat16)
        low = (scale - high.astype(jnp.float32)).astype(jnp.bfloat16)
        lane = lax.broadcasted_iota(jnp.int32, (high.shape[0], LANES), 1)
        sends[-1] = jnp.concatenate([sends[-1], jnp.where(lane == 0, high, low)], axis=1)
        for stage in reversed(range(devices.bit_length() - 1)):
            sends = [jnp.concatenate([block, exchange(block, stage, devices)], axis=0) for block in sends]
        tail = sends[-1][:, -LANES:].astype(jnp.float32)
        scale = tail[:, 0:1] + tail[:, 1:2]
        sends[-1] = sends[-1][:, :-LANES]
        gate_proj = up_proj = 0.0
        for rows, (lo, hi) in zip(sends, spans):
            gate_proj = gate_proj + jnp.dot(rows, gate_weight[lo:hi], preferred_element_type=jnp.float32)
            up_proj = up_proj + jnp.dot(rows, up_weight[lo:hi], preferred_element_type=jnp.float32)

        hidden = (jax.nn.gelu(gate_proj * scale, approximate=True) * (up_proj * scale)).astype(jnp.bfloat16)
        hidden = lax.optimization_barrier(hidden)

        rebuilt = jnp.concatenate(rebuilt, axis=1)
        spans = column_chunks(width, OUT_CHUNKS)
        sums = [jnp.dot(hidden, down_weight[:, lo:hi], preferred_element_type=jnp.float32) for lo, hi in spans]
        ffn_sum = scatter_all(sums, devices)
        ffn_sum = jnp.concatenate(ffn_sum, axis=1)
        scale = lax.rsqrt(jnp.mean(ffn_sum * ffn_sum, axis=-1, keepdims=True) + epsilon)
        return (rebuilt + ffn_sum * scale * post_gain).astype(jnp.bfloat16)

    return per_device


def solution(mesh):
    devices = mesh.shape[AXIS]
    return jax.shard_map(
        build(devices),
        mesh=mesh,
        in_specs=(
            P(("parts", AXIS), None),
            P(None, AXIS),
            P(AXIS),
            P(AXIS),
            P(AXIS, None),
            P(),
            P(),
            P(None, AXIS),
            P(None, AXIS),
            P(AXIS, None),
            P(),
        ),
        out_specs=P(("parts", AXIS), None),
        check_vma=False,
    )
```
